512 devices in a mesh: loop: 8 (over y_hi, x), inner: 64 (over z, y_lo, core).
Axes of the slice: x: 4, y: 4 (y_hi: 2, y_lo: 2; y = y_hi * 2 + y_lo), z: 16, core: 2. Of those that a mesh axis runs over, the one named last changes fastest.
Arguments:
- site_blocks: bfloat16 [8, 64, 4, 256, 256], P('loop', 'inner'), may hold values from -6 to 6
- bond_weights: float32 [8, 64, 256], P('loop', 'inner'), may hold values from 0.2 to 2
- bond_gates: float32 [8, 16, 16], P('loop'), may hold values from -3 to 3
- kept_slots: int32 [8, 64], P('loop', 'inner'), may hold values from 64 to 256, as said below
Outputs:
- new_sites: bfloat16 [8, 64, 4, 256, 256], P('loop', 'inner')
- new_weights: float32 [8, 64, 256], P('loop', 'inner')
The draws below stay inside these ranges and needn't reach their ends.
Inputs may be any that keep to these rules, and one draw needn't show every extreme that they name: `kept_slots`: every bond has at least one sector block with all 256 slots kept.
All inputs are finite; a program needn't handle non-finite values.
Results may differ from the reference program's by a relative error of at most 0.015.
The reference program's roundings to bfloat16 on the way count: a program that leaves them out, or rounds other values in their place, can miss the bound.
Values may be sent and summed in bfloat16 or wider, within the bound.
A program may use at most 64 MiB of HBM per device.

```python
import math
import jax
import jax.numpy as jnp
import numpy as np
from jax import lax

PHYS = 4
SB = 256
NSEC = 64
NSITE = 8


def draw_kept_slots(key, part):
    first_key, second_key = jax.random.split(jax.random.fold_in(key, 17))
    values = jax.random.randint(first_key, (NSITE, NSEC), SB // 4, SB + 1)
    spot = jax.random.randint(second_key, (NSITE, 1), 0, NSEC)
    column = jnp.arange(NSEC)[None, :]
    return jnp.where(column == spot, SB, values).astype(jnp.int32)


def block_levels(stream_key, shape, cuts, smallest, largest):
    gain, own = 1.0, jax.random.fold_in(stream_key, 6)
    for dim, parts in cuts:
        draws = jnp.exp(jax.random.uniform(jax.random.fold_in(own, dim), (parts,), jnp.float32, smallest / len(cuts), largest / len(cuts)))
        gain = gain * jnp.repeat(draws, shape[dim] // parts).reshape([-1 if axis == dim else 1 for axis in range(len(shape))])
    return gain


def bell_draw(stream_key, shape, scale, limit, cuts=(), kind=jnp.bfloat16):
    loudness = block_levels(stream_key, shape, cuts, -0.22, 0.18) if cuts else 1.0
    values = jax.random.normal(stream_key, shape, jnp.float32) * scale * loudness
    return jnp.minimum(jnp.maximum(values, -limit), limit).astype(kind)


def setup_inputs(seed: int = 0) -> dict:
    key_list = jax.random.split(jax.random.key(seed), 5)
    return {
        "site_blocks": bell_draw(key_list[0], (NSITE, NSEC, PHYS, SB, SB), 1.0, 6.0, ((0, 8), (1, 64))),
        "bond_weights": jnp.clip(jnp.exp(math.log(2.0) - 2.3025851 * jax.random.uniform(key_list[1], (NSITE, NSEC, SB), jnp.float32) ** block_levels(key_list[1], (NSITE, NSEC, SB), ((0, 8), (1, 64)), -0.2, 0.2)), 0.2, 2.0),
        "bond_gates": bell_draw(key_list[2], (NSITE, PHYS * PHYS, PHYS * PHYS), 0.5, 3.0, ((0, 8),), jnp.float32),
        "kept_slots": draw_kept_slots(jax.random.fold_in(key_list[4], 71), 0),
    }


CHARGE = np.array([0, 1, 1, 2])

def gate_masks():
    table = np.zeros((3, 16, 16), np.float32)
    for outer_a in range(4):
        for outer_b in range(4):
            for source_a in range(4):
                for source_b in range(4):
                    offset = CHARGE[source_a] - CHARGE[outer_a]
                    same_total = CHARGE[outer_a] + CHARGE[outer_b] == CHARGE[source_a] + CHARGE[source_b]
                    if same_total and offset >= -1 and (offset <= 1):
                        table[offset + 1, outer_a * 4 + outer_b, source_a * 4 + source_b] = 1.0
    return table

def rounded(values):
    return lax.optimization_barrier(values.astype(jnp.bfloat16))

def pair_products(scaled, pieces):
    products = jnp.einsum('mars,mbst->mabrt', scaled.astype(jnp.float32), pieces.astype(jnp.float32), precision=lax.Precision.HIGHEST)
    return rounded(products * (1.0 / math.sqrt(SB))).reshape(NSEC, PHYS * PHYS, SB, SB)

def bond_update(left_site, right_site, weight_row, gate_matrix, kept_row):
    row_count = PHYS * SB
    pieces = jnp.stack([jnp.roll(right_site[:, state], -int(CHARGE[state]), axis=0) for state in range(PHYS)], axis=1)
    scaled = rounded(left_site.astype(jnp.float32) * weight_row[:, None, None, :])
    theta_terms = pair_products(scaled, pieces).astype(jnp.float32)
    mixer_table = rounded(gate_matrix[None] * jnp.asarray(gate_masks())).astype(jnp.float32)
    mixed_terms = jnp.zeros((NSEC, PHYS * PHYS, SB, SB), jnp.float32)
    for position, offset in enumerate((-1, 0, 1)):
        source = jnp.roll(theta_terms, -offset, axis=0)
        mixed_terms = mixed_terms + jnp.einsum('kj,mjrs->mkrs', mixer_table[position], source, precision=lax.Precision.HIGHEST)
    mixed_terms = rounded(mixed_terms).astype(jnp.float32)
    matrix = mixed_terms.reshape(NSEC, PHYS, PHYS, SB, SB).transpose(0, 1, 3, 2, 4).reshape(NSEC, row_count, row_count)
    column = jnp.arange(SB)[None, None, None, :]
    old_basis = jnp.where(column < kept_row[:, None, None, None], left_site, jnp.zeros_like(left_site))
    old_basis = old_basis.astype(jnp.float32).reshape(NSEC, row_count, SB)
    projected = jnp.einsum('mij,mik->mjk', matrix, old_basis, precision=lax.Precision.HIGHEST)
    gram_matrix = jnp.einsum('mjk,mjl->mkl', projected, projected, precision=lax.Precision.HIGHEST) + jnp.eye(SB, dtype=jnp.float32)
    factor = jnp.linalg.cholesky(gram_matrix)
    solved = jax.vmap(lambda lower_part, right_part: jax.scipy.linalg.solve_triangular(lower_part, right_part, lower=True))(factor, jnp.swapaxes(projected, 1, 2))
    orthonormal = jnp.swapaxes(solved, 1, 2)
    isometry = rounded(orthonormal * math.sqrt(row_count))
    carried = jnp.einsum('mij,mjk->mik', matrix, isometry.astype(jnp.float32), precision=lax.Precision.HIGHEST) * (1.0 / math.sqrt(row_count))
    new_level = jnp.sqrt(lax.optimization_barrier(jnp.mean(carried * carried, axis=1)) + 1e-06)
    new_left = (carried / new_level[:, None, :]).astype(jnp.bfloat16).reshape(NSEC, PHYS, SB, SB)
    right_parts = isometry.reshape(NSEC, PHYS, SB, SB).transpose(0, 1, 3, 2)
    new_right = jnp.stack([jnp.roll(right_parts[:, state], int(CHARGE[state]), axis=0) for state in range(PHYS)], axis=1)
    return (new_left, new_level, new_right)

def reference(site_blocks, bond_weights, bond_gates, kept_slots):
    sites = [site_blocks[position] for position in range(NSITE)]
    levels = [bond_weights[position] for position in range(NSITE)]
    for parity in (0, 1):
        for left_index in range(parity, NSITE, 2):
            right_index = (left_index + 1) % NSITE
            new_left, new_level, new_right = bond_update(sites[left_index], sites[right_index], levels[left_index], bond_gates[left_index], kept_slots[left_index])
            sites[left_index] = new_left
            sites[right_index] = new_right
            levels[left_index] = new_level
    results = []
    for position in range(NSITE):
        earlier = levels[(position - 1) % NSITE]
        row_scale = jnp.stack([jnp.roll(earlier, int(CHARGE[state]), axis=0) for state in range(PHYS)], axis=1)
        results.append((sites[position].astype(jnp.float32) * row_scale[:, :, :, None]).astype(jnp.bfloat16))
    return (jnp.stack(results), jnp.stack(levels))
```

```python
import functools

import jax
import jax.numpy as jnp
from jax import lax
from jax.experimental import pallas as pl
from jax.experimental.pallas import tpu as pltpu
from jax.sharding import PartitionSpec as P

HI = lax.Precision.HIGHEST
NN = (((1,), (0,)), ((), ()))
NT = (((1,), (1,)), ((), ()))
MESH = pl.DeviceIdType.MESH
SLOTS = 256
CHARGE = (0, 1, 1, 2)

LEFT_AT = {-1: {0: 0, 1: 1, 2: 2}, 0: {0: 3, 1: 4, 2: 5, 3: 6}, 1: {1: 7, 2: 8, 3: 9}}
RIGHT_AT = {-1: {1: 1, 2: 2, 3: 6}, 0: {0: 0, 1: 4, 2: 5, 3: 9}, 1: {0: 3, 1: 7, 2: 8}}
PAIRS = [(d, a, b) for d in (-1, 0, 1) for a in LEFT_AT[d] for b in RIGHT_AT[d]]
THETA_AT = {key: n for n, key in enumerate(PAIRS)}


def even(number):
    return 1 - number % 2


def sends(phase, loop, inner):
    home = lambda bond, sector: (bond + even(sector), sector)
    bond = loop - even(inner)
    found = []
    if phase == 0:
        for slot, step in enumerate((1, 0, -1)):
            found.append(("meta_in", 0, 8, "meta", 8 * slot, home(loop, inner + step)))
        if loop % 2 == 0:
            for step, at, size, to in ((1, 0, 3, 0), (0, 0, 4, 3), (-1, 1, 3, 7)):
                found.append(("site", at, size, "left", to, home(loop, inner + step)))
        else:
            for step, at, size, to in ((0, 0, 3, 0), (-1, 0, 4, 3), (-2, 1, 3, 7)):
                found.append(("site", at, size, "right", to, home(loop - 1, inner + step)))
    elif phase == 1 and bond % 2 == 0:
        for step, at, size, to in ((0, 0, 1, 3), (0, 1, 2, 7), (1, 0, 1, 0), (1, 1, 2, 4), (1, 3, 1, 9), (2, 1, 2, 1), (2, 3, 1, 6)):
            found.append(("new_right", at, size, "left", to, home(bond + 1, inner + step)))
        for step, at, size, to in ((0, 0, 3, 0), (-1, 0, 4, 3), (-2, 1, 3, 7)):
            found.append(("new_left", at, size, "right", to, home(bond - 1, inner + step)))
        for step in (0, 1, 2):
            found.append(("level", 0, 8, "levels", 8 * step, home(bond + 1, inner + step)))
        found.append(("level", 0, 8, "weights", 0, (bond, inner)))
    elif phase == 2 and bond % 2 == 1:
        found.append(("new_left", 0, 4, "sites", 0, (bond, inner)))
        for step, at, size in ((0, 0, 1), (1, 1, 2), (2, 3, 1)):
            found.append(("new_right", at, size, "sites", at, (bond + 1, inner + step)))
        found.append(("level", 0, 8, "weights", 0, (bond, inner)))
    if phase == 2 and loop % 2 == 0:
        found.append(("early", 0, 8, "weights", 0, (loop, inner)))
    return [f[:5] + ((f[5][0] - loop, f[5][1] - inner),) for f in found]


def arrivals(phase, loop, inner):
    found = []
    for far in range(-3, 4):
        for away in range(-3, 4):
            for _, _, size, to, at, (x, y) in sends(phase, loop + far, inner + away):
                if (far + x, away + y) == (0, 0):
                    found.append((to, at, size, (far, away)))
    return found


def landings(phase):
    spots = set()
    for kind in range(4):
        spots |= {a[:3] for a in arrivals(phase, 4 + kind // 2, 4 + kind % 2)}
    return sorted(spots)


def partners(phase, loop, inner):
    known = {s[5] for s in sends(phase, loop, inner)} | {a[3] for a in arrivals(phase, loop, inner)}
    return sorted(known - {(0, 0)})


def exchange(phase, refs, barrier, send_sems, recv_sems):
    loop, inner = lax.axis_index("loop"), lax.axis_index("inner")
    rounds, sectors = lax.axis_size("loop"), lax.axis_size("inner")
    spots = landings(phase)

    def device(offset):
        return (lax.rem(loop + offset[0] + rounds, rounds), lax.rem(inner + offset[1] + sectors, sectors))

    for kind in range(4):
        at = (4 + kind // 2, 4 + kind % 2)

        @pl.when((lax.rem(loop, 2) == kind // 2) & (lax.rem(inner, 2) == kind % 2))
        def _(at=at):
            friends = partners(phase, *at)
            for offset in friends:
                pl.semaphore_signal(barrier, inc=1, device_id=device(offset), device_id_type=MESH)
            pl.semaphore_wait(barrier, len(friends))
            copies = []
            for n, (source, first, size, to, where, offset) in enumerate(sends(phase, *at)):
                src, dst = refs[source].at[pl.ds(first, size)], refs[to].at[pl.ds(where, size)]
                slot = recv_sems.at[spots.index((to, where, size))]
                if offset == (0, 0):
                    copy = pltpu.make_async_copy(src, dst, slot)
                else:
                    copy = pltpu.make_async_remote_copy(src, dst, send_sems.at[n], slot, device_id=device(offset), device_id_type=MESH)
                    copies.append(copy)
                copy.start()
            for to, where, size, offset in arrivals(phase, *at):
                dst = refs[to].at[pl.ds(where, size)]
                pltpu.make_async_copy(dst, dst, recv_sems.at[spots.index((to, where, size))]).wait()
            for copy in copies:
                copy.wait_send()


def exchange_call(phase, sources, targets):
    names, shapes = list(sources), list(targets)

    def body(*refs):
        exchange(phase, dict(zip(names + shapes, refs)), pltpu.get_barrier_semaphore(), *refs[-2:])

    most = max(len(sends(phase, 4 + kind // 2, 4 + kind % 2)) for kind in range(4))
    results = pl.pallas_call(
        body,
        out_shape=tuple(targets.values()),
        in_specs=[pl.BlockSpec(memory_space=pl.ANY)] * len(names),
        out_specs=tuple([pl.BlockSpec(memory_space=pl.ANY)] * len(shapes)),
        scratch_shapes=[pltpu.SemaphoreType.DMA((most,)), pltpu.SemaphoreType.DMA((len(landings(phase)),))],
        compiler_params=pltpu.CompilerParams(collective_id=phase, has_side_effects=True),
    )(*sources.values())
    return dict(zip(shapes, results))


def terms_of(outer_a, outer_b):
    found = []
    for d, a, b in PAIRS:
        if CHARGE[a] - CHARGE[outer_a] == d and CHARGE[outer_b] - CHARGE[b] == d:
            found.append(((outer_a * 4 + outer_b) * 16 + a * 4 + b, THETA_AT[d, a, b]))
    return found


def invert_leaf(work):
    n = 128
    lane = lax.broadcasted_iota(jnp.int32, (8, n), 1)
    sub = lax.broadcasted_iota(jnp.int32, (8, n), 0)
    tiles = [work[8 * t:8 * t + 8, :] for t in range(n // 8)]
    for g in range(n // 8):
        k = 8 * g
        cols = {}
        for t in range(g, n // 8):
            cols[t] = [jnp.broadcast_to(tiles[t][:, k + j:k + j + 1], (8, n)) for j in range(8)]
        fresh = (lane >= k) & (lane < k + 8)
        head = jnp.where(fresh, jnp.where(lane - k == sub, 1.0, 0.0), tiles[g])
        for t in range(g + 1, n // 8):
            tiles[t] = jnp.where(fresh, 0.0, tiles[t])
        rows = []
        for j in range(8):
            scale = lax.rsqrt(jnp.broadcast_to(cols[g][j][j:j + 1, :], (8, n)))
            for t in range(g, n // 8):
                cols[t][j] = cols[t][j] * scale
            low = jnp.where(sub > j, cols[g][j], 0.0)
            for i in range(j + 1, 8):
                other = jnp.broadcast_to(low[i:i + 1, :], (8, n))
                for t in range(g, n // 8):
                    cols[t][i] = cols[t][i] - (low if t == g else cols[t][j]) * other
            row = jnp.broadcast_to(head[j:j + 1, :], (8, n)) * scale
            rows.append(row)
            head = jnp.where(sub == j, row, head - low * row)
        for t in range(g + 1, n // 8):
            total = tiles[t]
            for j in range(8):
                total = total - cols[t][j] * rows[j]
            tiles[t] = total
        work[8 * g:8 * g + 8, :] = jnp.where(lane <= sub + k, head, 0.0)


def task(last, meta, left, right, levels, new_left, new_right, level, theta, matrix, proj, gram, work, scaled, numbers, sem):
    n = SLOTS
    copy = pltpu.make_async_copy(meta.at[pl.ds(8, 8)], numbers, sem)
    copy.start()
    for d, at in LEFT_AT.items():
        row = meta[8 * (d + 1):8 * (d + 1) + 1, :]
        for k in at.values():
            scaled[k] = (left[k].astype(jnp.float32) * row).astype(jnp.bfloat16)
    for d, a, b in PAIRS:
        product = jnp.dot(scaled[LEFT_AT[d][a]], right[RIGHT_AT[d][b]], preferred_element_type=jnp.float32)
        theta[THETA_AT[d, a, b]] = (product * (1.0 / 16.0)).astype(jnp.bfloat16)
    copy.wait()

    @pl.loop(0, n // 16)
    def _(step):
        r = pl.multiple_of(step * 16, 16)
        for a in range(4):
            for b in range(4):
                total = None
                for g, t in terms_of(a, b):
                    term = theta[t, pl.ds(r, 16), :].astype(jnp.float32) * numbers[2, g]
                    total = term if total is None else total + term
                matrix[pl.ds(pl.multiple_of(a * n + r, 16), 16), b * n:(b + 1) * n] = total.astype(jnp.bfloat16)

    down = lax.broadcasted_iota(jnp.int32, (n, n), 0)
    diagonal = down == lax.broadcasted_iota(jnp.int32, (n, n), 1)
    total = None
    for a in range(4):
        part = jnp.dot(left[3 + a].T, matrix[a * n:(a + 1) * n, :], preferred_element_type=jnp.float32)
        total = part if total is None else total + part
    row_number = lax.broadcasted_iota(jnp.int32, (n, 4 * n), 0).astype(jnp.float32)
    proj[...] = jnp.where(row_number < numbers[1, 0], total, 0.0)
    dot = functools.partial(lax.dot_general, precision=HI, preferred_element_type=jnp.float32)
    gram[...] = dot(proj[...], proj[...], NT) + jnp.where(diagonal, 1.0, 0.0)
    h = n // 2
    work[...] = gram[:h, :h]
    invert_leaf(work)
    first = work[...]
    lower = dot(gram[h:, :h], first, NT)
    top = dot(first, proj[:h, :], NN)
    work[...] = gram[h:, h:] - dot(lower, lower, NT)
    proj[h:, :] = proj[h:, :] - dot(lower, top, NN)
    proj[:h, :] = top
    invert_leaf(work)
    proj[h:, :] = dot(work[...], proj[h:, :], NN)
    iso = (proj[...] * 32.0).astype(jnp.bfloat16)
    carried = []
    squares = jnp.zeros((1, n), jnp.float32)
    for a in range(4):
        part = lax.dot_general(matrix[a * n:(a + 1) * n, :], iso, NT, preferred_element_type=jnp.float32) * (1.0 / 32.0)
        carried.append(part)
        squares = squares + jnp.sum(part * part, axis=0, keepdims=True)
    lev = jnp.sqrt(squares * (1.0 / 1024.0) + 1e-6)
    level[...] = jnp.broadcast_to(lev, (8, n))

    def upright(row):
        return jnp.sum(jnp.where(diagonal, row, 0.0), axis=1, keepdims=True)

    right_scale = upright(lev) if last else None
    for a in range(4):
        block = (carried[a] / lev).astype(jnp.bfloat16)
        other = iso[:, a * n:(a + 1) * n]
        if last:
            block = (block.astype(jnp.float32) * upright(levels[8 * CHARGE[a]:8 * CHARGE[a] + 1, :])).astype(jnp.bfloat16)
            other = (other.astype(jnp.float32) * right_scale).astype(jnp.bfloat16)
        new_left[a] = block
        new_right[a] = other


def task_call(last, meta, left, right, levels):
    def body(meta, left, right, levels, *others):
        @pl.when(lax.rem(lax.axis_index("loop") + lax.axis_index("inner"), 2) == (0 if last else 1))
        def _():
            task(last, meta, left, right, levels, *others)

    vmem = pl.BlockSpec(memory_space=pltpu.VMEM)
    n = SLOTS
    results = pl.pallas_call(
        body,
        out_shape=(
            jax.ShapeDtypeStruct((4, n, n), jnp.bfloat16),
            jax.ShapeDtypeStruct((4, n, n), jnp.bfloat16),
            jax.ShapeDtypeStruct((8, n), jnp.float32),
        ),
        in_specs=[vmem] * 4,
        out_specs=(vmem,) * 3,
        scratch_shapes=[
            pltpu.VMEM((len(PAIRS), n, n), jnp.bfloat16),
            pltpu.VMEM((4 * n, 4 * n), jnp.bfloat16),
            pltpu.VMEM((n, 4 * n), jnp.float32),
            pltpu.VMEM((n, n), jnp.float32),
            pltpu.VMEM((n // 2, n // 2), jnp.float32),
            pltpu.VMEM((10, n, n), jnp.bfloat16),
            pltpu.SMEM((8, n), jnp.float32),
            pltpu.SemaphoreType.DMA,
        ],
        compiler_params=pltpu.CompilerParams(vmem_limit_bytes=48 << 20),
    )(meta, left, right, levels)
    return dict(zip(("new_left", "new_right", "level"), results))


def per_device(site_blocks, bond_weights, bond_gates, kept_slots):
    n = SLOTS
    gates = lax.reduce_precision(bond_gates.reshape(1, n), 8, 7)
    kept = jnp.broadcast_to(kept_slots.astype(jnp.float32), (1, n))
    meta = jnp.concatenate([bond_weights[0], kept, gates, jnp.zeros((5, n), jnp.float32)], axis=0)
    blocks = lambda count: jax.ShapeDtypeStruct((count, n, n), jnp.bfloat16)
    rows = lambda count: jax.ShapeDtypeStruct((count, n), jnp.float32)
    got = exchange_call(0, {"site": site_blocks[0, 0], "meta_in": meta}, {"left": blocks(10), "right": blocks(10), "meta": rows(24)})
    first = task_call(False, got["meta"], got["left"], got["right"], got["meta"])
    then = exchange_call(1, first, {"left": blocks(10), "right": blocks(10), "levels": rows(24), "weights": rows(8)})
    second = task_call(True, got["meta"], then["left"], then["right"], then["levels"])
    second["early"] = then["weights"]
    final = exchange_call(2, second, {"sites": blocks(4), "weights": rows(8)})
    return (final["sites"][None, None], final["weights"][None, :1])


def solution(mesh):
    return jax.shard_map(
        per_device,
        mesh=mesh,
        in_specs=(
            P("loop", "inner", None, None, None),
            P("loop", "inner", None),
            P("loop", None, None),
            P("loop", "inner"),
        ),
        out_specs=(P("loop", "inner", None, None, None), P("loop", "inner", None)),
        check_vma=False,
    )
```

```python
import functools

import jax
import jax.numpy as jnp
from jax import lax
from jax.experimental import pallas as pl
from jax.experimental.pallas import tpu as pltpu
from jax.sharding import PartitionSpec as P

HI = lax.Precision.HIGHEST
NN = (((1,), (0,)), ((), ()))
NT = (((1,), (1,)), ((), ()))
MESH = pl.DeviceIdType.MESH
SLOTS = 256
CHARGE = (0, 1, 1, 2)

LEFT_AT = {-1: {0: 0, 1: 1, 2: 2}, 0: {0: 3, 1: 4, 2: 5, 3: 6}, 1: {1: 7, 2: 8, 3: 9}}
RIGHT_AT = {-1: {1: 1, 2: 2, 3: 6}, 0: {0: 0, 1: 4, 2: 5, 3: 9}, 1: {0: 3, 1: 7, 2: 8}}
PAIRS = [(d, a, b) for d in (-1, 0, 1) for a in LEFT_AT[d] for b in RIGHT_AT[d]]
THETA_AT = {key: n for n, key in enumerate(PAIRS)}


def even(number):
    return 1 - number % 2


def sends(phase, loop, inner):
    home = lambda bond, sector: (bond + even(sector), sector)
    bond = loop - even(inner)
    found = []
    if phase == 0:
        if loop % 2 == 0:
            for step, at, size, to in ((-1, 1, 3, 7), (1, 0, 3, 0), (0, 0, 4, 3)):
                found.append(("site", at, size, "left", to, home(loop, inner + step)))
        else:
            for step, at, size, to in ((-2, 1, 3, 7), (-1, 0, 4, 3), (0, 0, 3, 0)):
                found.append(("site", at, size, "right", to, home(loop - 1, inner + step)))
        for slot, step in enumerate((1, 0, -1)):
            found.append(("notes", 0, 24, "meta", 24 * slot, home(loop, inner + step)))
    elif phase == 1 and bond % 2 == 0:
        for step, at, size, to in ((2, 1, 2, 1), (2, 3, 1, 6), (1, 0, 1, 0), (1, 1, 2, 4), (1, 3, 1, 9), (0, 0, 1, 3), (0, 1, 2, 7)):
            found.append(("new_right", at, size, "left", to, home(bond + 1, inner + step)))
    elif phase == 2 and bond % 2 == 0:
        for step in (0, 1, 2):
            found.append(("level", 0, 8, "levels", 8 * step, home(bond + 1, inner + step)))
        found.append(("level", 0, 8, "weights", 0, (bond, inner)))
        for step, at, size, to in ((-2, 1, 3, 7), (-1, 0, 4, 3), (0, 0, 3, 0)):
            found.append(("new_left", at, size, "right", to, home(bond - 1, inner + step)))
    elif phase == 2 and bond % 2 == 1:
        found.append(("level", 0, 8, "weights", 0, (bond, inner)))
        found.append(("new_left", 0, 4, "sites", 0, (bond, inner)))
        for step, at, size in ((2, 3, 1), (1, 1, 2), (0, 0, 1)):
            found.append(("new_right", at, size, "sites", at, (bond + 1, inner + step)))
    return [f[:5] + ((f[5][0] - loop, f[5][1] - inner),) for f in found]


def arrivals(phase, loop, inner):
    found = []
    for far in range(-3, 4):
        for away in range(-3, 4):
            for _, _, size, to, at, (x, y) in sends(phase, loop + far, inner + away):
                if (far + x, away + y) == (0, 0):
                    found.append((to, at, size, (far, away)))
    return found


def kind_of(kind):
    return (4 + kind // 2, 4 + kind % 2)


PHASES = (0, 1, 2)
LANDINGS = sorted({a[:3] for phase in PHASES for kind in range(4) for a in arrivals(phase, *kind_of(kind))})
MOST = max(sum(len(sends(phase, *kind_of(kind))) for phase in PHASES) for kind in range(4))


def partners(loop, inner):
    known = {s[5] for phase in PHASES for s in sends(phase, loop, inner)}
    known |= {a[3] for phase in PHASES for a in arrivals(phase, loop, inner)}
    return sorted(known - {(0, 0)})


def by_kind(work):
    loop, inner = lax.axis_index("loop"), lax.axis_index("inner")
    for kind in range(4):
        pl.when((lax.rem(loop, 2) == kind // 2) & (lax.rem(inner, 2) == kind % 2))(functools.partial(work, kind))


def device(offset):
    loop, inner = lax.axis_index("loop"), lax.axis_index("inner")
    rounds, sectors = lax.axis_size("loop"), lax.axis_size("inner")
    return (lax.rem(loop + offset[0] + rounds, rounds), lax.rem(inner + offset[1] + sectors, sectors))


def greet(barrier, kind):
    friends = partners(*kind_of(kind))
    for offset in friends:
        pl.semaphore_signal(barrier, inc=1, device_id=device(offset), device_id_type=MESH)
    pl.semaphore_wait(barrier, len(friends))


def outgoing(phase, refs, send_sems, recv_sems, kind):
    first = sum(len(sends(p, *kind_of(kind))) for p in range(phase))
    copies = []
    for n, (source, at, size, to, where, offset) in enumerate(sends(phase, *kind_of(kind))):
        src, dst = refs[source].at[pl.ds(at, size)], refs[to].at[pl.ds(where, size)]
        slot = recv_sems.at[LANDINGS.index((to, where, size))]
        if offset == (0, 0):
            copies.append((None, pltpu.make_async_copy(src, dst, slot)))
        else:
            sem = send_sems.at[first + n]
            copies.append((sem, pltpu.make_async_remote_copy(src, dst, sem, slot, device_id=device(offset), device_id_type=MESH)))
    return copies


def start(phase, refs, send_sems, recv_sems, kind):
    for _, copy in outgoing(phase, refs, send_sems, recv_sems, kind):
        copy.start()


def finish(refs, send_sems, recv_sems, kind):
    for phase in PHASES:
        for sem, copy in outgoing(phase, refs, send_sems, recv_sems, kind):
            if sem is not None:
                copy.wait_send()


def expect(buffers, refs, recv_sems, kind):
    for phase in PHASES:
        for to, where, size, _ in arrivals(phase, *kind_of(kind)):
            if to in buffers:
                dst = refs[to].at[pl.ds(where, size)]
                pltpu.make_async_copy(dst, dst, recv_sems.at[LANDINGS.index((to, where, size))]).wait()


def terms_of(outer_a, outer_b):
    found = []
    for d, a, b in PAIRS:
        if CHARGE[a] - CHARGE[outer_a] == d and CHARGE[outer_b] - CHARGE[b] == d:
            found.append(((outer_a * 4 + outer_b) * 16 + a * 4 + b, THETA_AT[d, a, b]))
    return found


def invert_leaf(work):
    n = 128
    lane = lax.broadcasted_iota(jnp.int32, (8, n), 1)
    sub = lax.broadcasted_iota(jnp.int32, (8, n), 0)
    tiles = [work[8 * t:8 * t + 8, :] for t in range(n // 8)]
    for g in range(n // 8):
        k = 8 * g
        cols = {}
        for t in range(g, n // 8):
            cols[t] = [jnp.broadcast_to(tiles[t][:, k + j:k + j + 1], (8, n)) for j in range(8)]
        fresh = (lane >= k) & (lane < k + 8)
        head = jnp.where(fresh, jnp.where(lane - k == sub, 1.0, 0.0), tiles[g])
        for t in range(g + 1, n // 8):
            tiles[t] = jnp.where(fresh, 0.0, tiles[t])
        rows = []
        for j in range(8):
            scale = lax.rsqrt(jnp.broadcast_to(cols[g][j][j:j + 1, :], (8, n)))
            for t in range(g, n // 8):
                cols[t][j] = cols[t][j] * scale
            low = jnp.where(sub > j, cols[g][j], 0.0)
            for i in range(j + 1, 8):
                other = jnp.broadcast_to(low[i:i + 1, :], (8, n))
                for t in range(g, n // 8):
                    cols[t][i] = cols[t][i] - (low if t == g else cols[t][j]) * other
            row = jnp.broadcast_to(head[j:j + 1, :], (8, n)) * scale
            rows.append(row)
            head = jnp.where(sub == j, row, head - low * row)
        for t in range(g + 1, n // 8):
            total = tiles[t]
            for j in range(8):
                total = total - cols[t][j] * rows[j]
            tiles[t] = total
        work[8 * g:8 * g + 8, :] = jnp.where(lane <= sub + k, head, 0.0)


def body(site, weights_in, gates_in, kept_in, sites, weights_out, left, right, meta, levels, weights, notes, new_left, new_right,
         level, theta, matrix, proj, gram, work, scaled, numbers, send_sems, recv_sems, sem):
    n = SLOTS
    refs = dict(site=site.at[0, 0], sites=sites.at[0, 0], left=left, right=right, meta=meta, levels=levels, weights=weights,
                notes=notes, new_left=new_left, new_right=new_right, level=level)
    state = (refs, send_sems, recv_sems)
    last = lax.rem(lax.axis_index("loop") + lax.axis_index("inner"), 2) == 0
    notes[0:8, :] = jnp.broadcast_to(weights_in[0], (8, n))
    gates = gates_in[0].astype(jnp.bfloat16).astype(jnp.float32)
    notes[8:24, :] = jnp.pad(gates, ((0, 0), (0, n - 16)))
    notes[7:8, :] = jnp.full((1, n), kept_in[0, 0].astype(jnp.float32))
    levels[...] = jnp.ones_like(levels)
    barrier = pltpu.get_barrier_semaphore()

    @by_kind
    def _(kind):
        greet(barrier, kind)
        start(0, *state, kind)
        expect(("meta",), refs, recv_sems, kind)
        expect(("left",), refs, recv_sems, kind)

    copy = pltpu.make_async_copy(meta.at[pl.ds(24, 24)], numbers, sem)
    copy.start()
    for d, at in LEFT_AT.items():
        row = meta[24 * (d + 1):24 * (d + 1) + 1, :]
        for k in at.values():
            scaled[k] = (left[k].astype(jnp.float32) * row).astype(jnp.bfloat16)

    @by_kind
    def _(kind):
        expect(("right",), refs, recv_sems, kind)

    for d, a, b in PAIRS:
        product = jnp.dot(scaled[LEFT_AT[d][a]], right[RIGHT_AT[d][b]], preferred_element_type=jnp.float32)
        theta[THETA_AT[d, a, b]] = (product * (1.0 / 16.0)).astype(jnp.bfloat16)
    copy.wait()

    @pl.loop(0, n // 16)
    def _(step):
        r = pl.multiple_of(step * 16, 16)
        for a in range(4):
            for b in range(4):
                total = None
                for g, t in terms_of(a, b):
                    term = theta[t, pl.ds(r, 16), :].astype(jnp.float32) * numbers[8 + g // 16, g % 16]
                    total = term if total is None else total + term
                matrix[pl.ds(pl.multiple_of(a * n + r, 16), 16), b * n:(b + 1) * n] = total.astype(jnp.bfloat16)

    down = lax.broadcasted_iota(jnp.int32, (n, n), 0)
    diagonal = down == lax.broadcasted_iota(jnp.int32, (n, n), 1)
    total = None
    for a in range(4):
        part = jnp.dot(left[3 + a].T, matrix[a * n:(a + 1) * n, :], preferred_element_type=jnp.float32)
        total = part if total is None else total + part
    row_number = lax.broadcasted_iota(jnp.int32, (n, 4 * n), 0).astype(jnp.float32)
    proj[...] = jnp.where(row_number < numbers[7, 0], total, 0.0)
    dot = functools.partial(lax.dot_general, precision=HI, preferred_element_type=jnp.float32)
    gram[...] = dot(proj[...], proj[...], NT) + jnp.where(diagonal, 1.0, 0.0)
    h = n // 2
    work[...] = gram[:h, :h]
    invert_leaf(work)
    first = work[...]
    lower = dot(gram[h:, :h], first, NT)
    top = dot(first, proj[:h, :], NN)
    work[...] = gram[h:, h:] - dot(lower, lower, NT)
    proj[h:, :] = proj[h:, :] - dot(lower, top, NN)
    proj[:h, :] = top
    invert_leaf(work)
    proj[h:, :] = dot(work[...], proj[h:, :], NN)
    iso = (proj[...] * 32.0).astype(jnp.bfloat16)
    for a in range(4):
        new_right[a] = iso[:, a * n:(a + 1) * n]

    @by_kind
    def _(kind):
        start(1, *state, kind)

    carried = []
    squares = jnp.zeros((1, n), jnp.float32)
    for a in range(4):
        part = lax.dot_general(matrix[a * n:(a + 1) * n, :], iso, NT, preferred_element_type=jnp.float32) * (1.0 / 32.0)
        carried.append(part)
        squares = squares + jnp.sum(part * part, axis=0, keepdims=True)
    lev = jnp.sqrt(squares * (1.0 / 1024.0) + 1e-6)
    level[...] = jnp.broadcast_to(lev, (8, n))

    def upright(row):
        return jnp.sum(jnp.where(diagonal, row, 0.0), axis=1, keepdims=True)

    @by_kind
    def _(kind):
        expect(("levels",), refs, recv_sems, kind)

    for a in range(4):
        block = (carried[a] / lev).astype(jnp.bfloat16).astype(jnp.float32)
        new_left[a] = (block * upright(levels[8 * CHARGE[a]:8 * CHARGE[a] + 1, :])).astype(jnp.bfloat16)

    @pl.when(last)
    def _():
        scale = upright(lev)
        for a in range(4):
            new_right[a] = (new_right[a].astype(jnp.float32) * scale).astype(jnp.bfloat16)

    @by_kind
    def _(kind):
        start(2, *state, kind)
        expect(("weights", "sites"), refs, recv_sems, kind)
        finish(*state, kind)

    weights_out[0] = weights[0:1, :]


def per_device(site_blocks, bond_weights, bond_gates, kept_slots):
    n = SLOTS
    vmem = pl.BlockSpec(memory_space=pltpu.VMEM)
    blocks = lambda count: pltpu.VMEM((count, n, n), jnp.bfloat16)
    rows = lambda count: pltpu.VMEM((count, n), jnp.float32)
    return pl.pallas_call(
        body,
        out_shape=(
            jax.ShapeDtypeStruct(site_blocks.shape, jnp.bfloat16),
            jax.ShapeDtypeStruct(bond_weights.shape, jnp.float32),
        ),
        in_specs=[pl.BlockSpec(memory_space=pl.ANY), vmem, vmem, pl.BlockSpec(memory_space=pltpu.SMEM)],
        out_specs=(pl.BlockSpec(memory_space=pl.ANY), vmem),
        scratch_shapes=[
            blocks(10), blocks(10), rows(72), rows(24), rows(8), rows(24), blocks(4), blocks(4), rows(8),
            blocks(len(PAIRS)),
            pltpu.VMEM((4 * n, 4 * n), jnp.bfloat16),
            pltpu.VMEM((n, 4 * n), jnp.float32),
            pltpu.VMEM((n, n), jnp.float32),
            pltpu.VMEM((n // 2, n // 2), jnp.float32),
            blocks(10),
            pltpu.SMEM((24, n), jnp.float32),
            pltpu.SemaphoreType.DMA((MOST,)),
            pltpu.SemaphoreType.DMA((len(LANDINGS),)),
            pltpu.SemaphoreType.DMA,
        ],
        compiler_params=pltpu.CompilerParams(collective_id=0, has_side_effects=True, vmem_limit_bytes=40 << 20),
    )(site_blocks, bond_weights, bond_gates, kept_slots)


def solution(mesh):
    return jax.shard_map(
        per_device,
        mesh=mesh,
        in_specs=(
            P("loop", "inner", None, None, None),
            P("loop", "inner", None),
            P("loop", None, None),
            P("loop", "inner"),
        ),
        out_specs=(P("loop", "inner", None, None, None), P("loop", "inner", None)),
        check_vma=False,
    )
```

```python
import functools

import jax
import jax.numpy as jnp
from jax import lax
from jax.experimental import pallas as pl
from jax.experimental.pallas import tpu as pltpu
from jax.sharding import PartitionSpec as P

HI = lax.Precision.HIGHEST
NN = (((1,), (0,)), ((), ()))
NT = (((1,), (1,)), ((), ()))
MESH = pl.DeviceIdType.MESH
SLOTS = 256
CHARGE = (0, 1, 1, 2)

LEFT_AT = {-1: {0: 0, 1: 1, 2: 2}, 0: {0: 3, 1: 4, 2: 5, 3: 6}, 1: {1: 7, 2: 8, 3: 9}}
RIGHT_AT = {-1: {1: 1, 2: 2, 3: 6}, 0: {0: 0, 1: 4, 2: 5, 3: 9}, 1: {0: 3, 1: 7, 2: 8}}
PAIRS = [(d, a, b) for d in (-1, 0, 1) for a in LEFT_AT[d] for b in RIGHT_AT[d]]
THETA_AT = {key: n for n, key in enumerate(PAIRS)}


def even(number):
    return 1 - number % 2


def sends(phase, loop, inner):
    home = lambda bond, sector: (bond + even(sector), sector)
    bond = loop - even(inner)
    found = []
    if phase == 0:
        if loop % 2 == 0:
            for step, at, size, to in ((-1, 1, 3, 7), (1, 0, 3, 0), (0, 0, 4, 3)):
                found.append(("site", at, size, "left", to, None, home(loop, inner + step)))
        else:
            for step, at, size, to in ((-2, 1, 3, 7), (-1, 0, 4, 3), (0, 0, 3, 0)):
                found.append(("site", at, size, "right", to, None, home(loop - 1, inner + step)))
        for slot, step in enumerate((1, 0, -1)):
            found.append(("notes", 0, 24, "meta", 24 * slot, None, home(loop, inner + step)))
    elif bond % 2 == 0:
        half = (phase - 1) // 2
        if phase % 2 == 1:
            for step, at, size, to in ((2, 1, 2, 1), (2, 3, 1, 6), (1, 0, 1, 0), (1, 1, 2, 4), (1, 3, 1, 9), (0, 0, 1, 3), (0, 1, 2, 7)):
                found.append(("new_right", at, size, "left", to, half, home(bond + 1, inner + step)))
        else:
            if half == 1:
                for step in (0, 1, 2):
                    found.append(("level", 0, 8, "levels", 8 * step, None, home(bond + 1, inner + step)))
                found.append(("level", 0, 8, "weights", 0, None, (bond, inner)))
            for step, at, size, to in ((-2, 1, 3, 7), (-1, 0, 4, 3), (0, 0, 3, 0)):
                found.append(("new_left", at, size, "right", to, half, home(bond - 1, inner + step)))
    elif phase % 2 == 0:
        half = (phase - 1) // 2
        if half == 1:
            found.append(("level", 0, 8, "weights", 0, None, (bond, inner)))
        found.append(("new_left", 0, 4, "sites", 0, half, (bond, inner)))
        for step, at, size in ((2, 3, 1), (1, 1, 2), (0, 0, 1)):
            found.append(("new_right", at, size, "sites", at, half, (bond + 1, inner + step)))
    return [f[:6] + ((f[6][0] - loop, f[6][1] - inner),) for f in found]


def spot_of(source, size, to, where, half):
    return (to, where, size, -1 if half is None else half, source == "new_right")


def part(ref, at, size, source, half):
    if half is None:
        return ref.at[pl.ds(at, size)]
    span = pl.ds(half * (SLOTS // 2), SLOTS // 2)
    return ref.at[pl.ds(at, size), span, :] if source == "new_right" else ref.at[pl.ds(at, size), :, span]


def arrivals(phase, loop, inner):
    found = []
    for far in range(-3, 4):
        for away in range(-3, 4):
            for source, _, size, to, at, half, (x, y) in sends(phase, loop + far, inner + away):
                if (far + x, away + y) == (0, 0):
                    found.append((source, to, at, size, half, (far, away)))
    return found


def kind_of(kind):
    return (4 + kind // 2, 4 + kind % 2)


PHASES = (0, 1, 2, 3, 4)
LANDINGS = sorted({spot_of(a[0], a[3], a[1], a[2], a[4]) for phase in PHASES for kind in range(4) for a in arrivals(phase, *kind_of(kind))})
MOST = max(sum(len(sends(phase, *kind_of(kind))) for phase in PHASES) for kind in range(4))


def partners(loop, inner):
    known = {s[6] for phase in PHASES for s in sends(phase, loop, inner)}
    known |= {a[5] for phase in PHASES for a in arrivals(phase, loop, inner)}
    return sorted(known - {(0, 0)})


def by_kind(work):
    loop, inner = lax.axis_index("loop"), lax.axis_index("inner")
    for kind in range(4):
        pl.when((lax.rem(loop, 2) == kind // 2) & (lax.rem(inner, 2) == kind % 2))(functools.partial(work, kind))


def device(offset):
    loop, inner = lax.axis_index("loop"), lax.axis_index("inner")
    rounds, sectors = lax.axis_size("loop"), lax.axis_size("inner")
    return (lax.rem(loop + offset[0] + rounds, rounds), lax.rem(inner + offset[1] + sectors, sectors))


def greet(barrier, kind):
    friends = partners(*kind_of(kind))
    for offset in friends:
        pl.semaphore_signal(barrier, inc=1, device_id=device(offset), device_id_type=MESH)
    pl.semaphore_wait(barrier, len(friends))


def outgoing(phase, refs, send_sems, recv_sems, kind):
    first = sum(len(sends(p, *kind_of(kind))) for p in range(phase))
    for n, (source, at, size, to, where, half, offset) in enumerate(sends(phase, *kind_of(kind))):
        src, dst = part(refs[source], at, size, source, half), part(refs[to], where, size, source, half)
        slot = recv_sems.at[LANDINGS.index(spot_of(source, size, to, where, half))]
        sem = send_sems.at[first + n]
        yield src, dst, sem, slot, offset


def start(phase, refs, send_sems, recv_sems, kind):
    for src, dst, sem, slot, offset in outgoing(phase, refs, send_sems, recv_sems, kind):
        if offset == (0, 0):
            pltpu.make_async_copy(src, dst, slot).start()
        else:
            pltpu.make_async_remote_copy(src, dst, sem, slot, device_id=device(offset), device_id_type=MESH).start()


def finish(refs, send_sems, recv_sems, kind):
    for phase in PHASES:
        for src, dst, sem, slot, offset in outgoing(phase, refs, send_sems, recv_sems, kind):
            if offset != (0, 0):
                pltpu.make_async_remote_copy(src, dst, sem, slot, device_id=device(offset), device_id_type=MESH).wait_send()


def expect(buffers, refs, recv_sems, kind, halves=(None, 0, 1)):
    for phase in PHASES:
        for source, to, where, size, half, _ in arrivals(phase, *kind_of(kind)):
            if to in buffers and half in halves:
                dst = part(refs[to], where, size, source, half)
                pltpu.make_async_copy(dst, dst, recv_sems.at[LANDINGS.index(spot_of(source, size, to, where, half))]).wait()


def terms_of(outer_a, outer_b):
    found = []
    for d, a, b in PAIRS:
        if CHARGE[a] - CHARGE[outer_a] == d and CHARGE[outer_b] - CHARGE[b] == d:
            found.append(((outer_a * 4 + outer_b) * 16 + a * 4 + b, THETA_AT[d, a, b]))
    return found


def invert_leaf(work):
    n = 128
    lane = lax.broadcasted_iota(jnp.int32, (8, n), 1)
    sub = lax.broadcasted_iota(jnp.int32, (8, n), 0)
    tiles = [work[8 * t:8 * t + 8, :] for t in range(n // 8)]
    for g in range(n // 8):
        k = 8 * g
        cols = {}
        for t in range(g, n // 8):
            cols[t] = [jnp.broadcast_to(tiles[t][:, k + j:k + j + 1], (8, n)) for j in range(8)]
        fresh = (lane >= k) & (lane < k + 8)
        head = jnp.where(fresh, jnp.where(lane - k == sub, 1.0, 0.0), tiles[g])
        for t in range(g + 1, n // 8):
            tiles[t] = jnp.where(fresh, 0.0, tiles[t])
        rows = []
        for j in range(8):
            scale = lax.rsqrt(jnp.broadcast_to(cols[g][j][j:j + 1, :], (8, n)))
            for t in range(g, n // 8):
                cols[t][j] = cols[t][j] * scale
            low = jnp.where(sub > j, cols[g][j], 0.0)
            for i in range(j + 1, 8):
                other = jnp.broadcast_to(low[i:i + 1, :], (8, n))
                for t in range(g, n // 8):
                    cols[t][i] = cols[t][i] - (low if t == g else cols[t][j]) * other
            row = jnp.broadcast_to(head[j:j + 1, :], (8, n)) * scale
            rows.append(row)
            head = jnp.where(sub == j, row, head - low * row)
        for t in range(g + 1, n // 8):
            total = tiles[t]
            for j in range(8):
                total = total - cols[t][j] * rows[j]
            tiles[t] = total
        work[8 * g:8 * g + 8, :] = jnp.where(lane <= sub + k, head, 0.0)


def body(site, weights_in, gates_in, kept_in, sites, weights_out, left, right, meta, levels, weights, notes, new_left, new_right,
         level, theta, matrix, proj, gram, work, scaled, numbers, lines, table, send_sems, recv_sems, sems):
    n = SLOTS
    h = n // 2
    refs = dict(site=site.at[0, 0], sites=sites.at[0, 0], left=left, right=right, meta=meta, levels=levels, weights=weights,
                notes=notes, new_left=new_left, new_right=new_right, level=level)
    state = (refs, send_sems, recv_sems)
    last = lax.rem(lax.axis_index("loop") + lax.axis_index("inner"), 2) == 0
    small = [
        pltpu.make_async_copy(weights_in.at[0], lines, sems.at[0]),
        pltpu.make_async_copy(gates_in.at[0], table, sems.at[1]),
    ]
    for copy in small:
        copy.start()
    levels[...] = jnp.ones_like(levels)
    barrier = pltpu.get_barrier_semaphore()

    @by_kind
    def _(kind):
        for offset in partners(*kind_of(kind)):
            pl.semaphore_signal(barrier, inc=1, device_id=device(offset), device_id_type=MESH)

    for copy in small:
        copy.wait()
    notes[0:7, :] = jnp.broadcast_to(lines[...], (7, n))
    notes[7:8, :] = jnp.full((1, n), kept_in[0, 0].astype(jnp.float32))
    notes[8:24, :] = jnp.pad(table[...].astype(jnp.bfloat16).astype(jnp.float32), ((0, 0), (0, n - 16)))

    @by_kind
    def _(kind):
        pl.semaphore_wait(barrier, len(partners(*kind_of(kind))))
        start(0, *state, kind)
        expect(("meta",), refs, recv_sems, kind)

    copy = pltpu.make_async_copy(meta.at[pl.ds(24, 24)], numbers, sems.at[2])
    copy.start()

    @by_kind
    def _(kind):
        expect(("left",), refs, recv_sems, kind)

    for d, at in LEFT_AT.items():
        row = meta[24 * (d + 1):24 * (d + 1) + 1, :]
        for k in at.values():
            scaled[k] = (left[k].astype(jnp.float32) * row).astype(jnp.bfloat16)

    @by_kind
    def _(kind):
        expect(("right", "levels"), refs, recv_sems, kind)

    for d, a, b in PAIRS:
        product = jnp.dot(scaled[LEFT_AT[d][a]], right[RIGHT_AT[d][b]], preferred_element_type=jnp.float32)
        theta[THETA_AT[d, a, b]] = (product * (1.0 / 16.0)).astype(jnp.bfloat16)
    copy.wait()

    @pl.loop(0, n // 16)
    def _(step):
        r = pl.multiple_of(step * 16, 16)
        for a in range(4):
            for b in range(4):
                total = None
                for g, t in terms_of(a, b):
                    term = theta[t, pl.ds(r, 16), :].astype(jnp.float32) * numbers[8 + g // 16, g % 16]
                    total = term if total is None else total + term
                matrix[pl.ds(pl.multiple_of(a * n + r, 16), 16), b * n:(b + 1) * n] = total.astype(jnp.bfloat16)

    total = None
    for a in range(4):
        product = jnp.dot(left[3 + a].T, matrix[a * n:(a + 1) * n, :], preferred_element_type=jnp.float32)
        total = product if total is None else total + product
    row_number = lax.broadcasted_iota(jnp.int32, (n, 4 * n), 0).astype(jnp.float32)
    proj[...] = jnp.where(row_number < numbers[7, 0], total, 0.0)
    dot = functools.partial(lax.dot_general, precision=HI, preferred_element_type=jnp.float32)
    diagonal = lambda size: lax.broadcasted_iota(jnp.int32, (size, size), 0) == lax.broadcasted_iota(jnp.int32, (size, size), 1)
    upright = lambda row: jnp.sum(jnp.where(diagonal(row.shape[1]), row, 0.0), axis=1, keepdims=True)
    gram[...] = dot(proj[...], proj[...], NT) + jnp.where(diagonal(n), 1.0, 0.0)

    def right_half(half, ortho):
        iso = (ortho * 32.0).astype(jnp.bfloat16)
        for a in range(4):
            new_right[a, half * h:(half + 1) * h, :] = iso[:, a * n:(a + 1) * n]

        @by_kind
        def _(kind):
            start(1 + 2 * half, *state, kind)

        return iso

    def left_half(half, iso):
        span = slice(half * h, (half + 1) * h)
        carried = []
        squares = jnp.zeros((1, h), jnp.float32)
        for a in range(4):
            product = lax.dot_general(matrix[a * n:(a + 1) * n, :], iso, NT, preferred_element_type=jnp.float32) * (1.0 / 32.0)
            carried.append(product)
            squares = squares + jnp.sum(product * product, axis=0, keepdims=True)
        lev = jnp.sqrt(squares * (1.0 / 1024.0) + 1e-6)
        level[:, span] = jnp.broadcast_to(lev, (8, h))
        inverse = 1.0 / lev
        for a in range(4):
            block = (carried[a] * inverse).astype(jnp.bfloat16).astype(jnp.float32)
            new_left[a, :, span] = (block * upright(levels[8 * CHARGE[a]:8 * CHARGE[a] + 1, :])).astype(jnp.bfloat16)

        @pl.when(last)
        def _():
            scale = upright(lev)
            for a in range(4):
                new_right[a, span, :] = (new_right[a, span, :].astype(jnp.float32) * scale).astype(jnp.bfloat16)

        @by_kind
        def _(kind):
            start(2 + 2 * half, *state, kind)

    work[...] = gram[:h, :h]
    invert_leaf(work)
    first = work[...]
    top = dot(first, proj[:h, :], NN)
    top_iso = right_half(0, top)
    lower = dot(gram[h:, :h], first, NT)
    work[...] = gram[h:, h:] - dot(lower, lower, NT)
    proj[h:, :] = proj[h:, :] - dot(lower, top, NN)
    left_half(0, top_iso)
    invert_leaf(work)
    left_half(1, right_half(1, dot(work[...], proj[h:, :], NN)))

    @by_kind
    def _(kind):
        expect(("weights", "sites"), refs, recv_sems, kind)
        finish(*state, kind)

    weights_out[0] = weights[0:1, :]


def per_device(site_blocks, bond_weights, bond_gates, kept_slots):
    n = SLOTS
    vmem = pl.BlockSpec(memory_space=pltpu.VMEM)
    blocks = lambda count: pltpu.VMEM((count, n, n), jnp.bfloat16)
    rows = lambda count: pltpu.VMEM((count, n), jnp.float32)
    return pl.pallas_call(
        body,
        out_shape=(
            jax.ShapeDtypeStruct(site_blocks.shape, jnp.bfloat16),
            jax.ShapeDtypeStruct(bond_weights.shape, jnp.float32),
        ),
        in_specs=[pl.BlockSpec(memory_space=pltpu.HBM)] * 3 + [pl.BlockSpec(memory_space=pltpu.SMEM)],
        out_specs=(pl.BlockSpec(memory_space=pl.ANY), vmem),
        scratch_shapes=[
            blocks(10), blocks(10), rows(72), rows(24), rows(8), rows(24), blocks(4), blocks(4), rows(8),
            blocks(len(PAIRS)),
            pltpu.VMEM((4 * n, 4 * n), jnp.bfloat16),
            pltpu.VMEM((n, 4 * n), jnp.float32),
            pltpu.VMEM((n, n), jnp.float32),
            pltpu.VMEM((n // 2, n // 2), jnp.float32),
            blocks(10),
            pltpu.SMEM((24, n), jnp.float32),
            rows(1),
            pltpu.VMEM((16, 16), jnp.float32),
            pltpu.SemaphoreType.DMA((MOST,)),
            pltpu.SemaphoreType.DMA((len(LANDINGS),)),
            pltpu.SemaphoreType.DMA((3,)),
        ],
        compiler_params=pltpu.CompilerParams(collective_id=0, has_side_effects=True, vmem_limit_bytes=40 << 20),
    )(*[pltpu.with_memory_space_constraint(x, pltpu.HBM) for x in (site_blocks, bond_weights, bond_gates)], kept_slots)


def solution(mesh):
    return jax.shard_map(
        per_device,
        mesh=mesh,
        in_specs=(
            P("loop", "inner", None, None, None),
            P("loop", "inner", None),
            P("loop", None, None),
            P("loop", "inner"),
        ),
        out_specs=(P("loop", "inner", None, None, None), P("loop", "inner", None)),
        check_vma=False,
    )
```

```python
import functools

import jax
import jax.numpy as jnp
from jax import lax
from jax.experimental import pallas as pl
from jax.experimental.pallas import tpu as pltpu
from jax.sharding import PartitionSpec as P

HI = lax.Precision.HIGHEST
NN = (((1,), (0,)), ((), ()))
NT = (((1,), (1,)), ((), ()))
MESH = pl.DeviceIdType.MESH
SLOTS = 256
CHARGE = (0, 1, 1, 2)

LEFT_AT = {-1: {0: 0, 1: 1, 2: 2}, 0: {0: 3, 1: 4, 2: 5, 3: 6}, 1: {1: 7, 2: 8, 3: 9}}
RIGHT_AT = {-1: {1: 1, 2: 2, 3: 6}, 0: {0: 0, 1: 4, 2: 5, 3: 9}, 1: {0: 3, 1: 7, 2: 8}}
PAIRS = [(d, a, b) for d in (-1, 0, 1) for a in LEFT_AT[d] for b in RIGHT_AT[d]]
THETA_AT = {key: n for n, key in enumerate(PAIRS)}


def even(number):
    return 1 - number % 2


def sends(phase, loop, inner):
    home = lambda bond, sector: (bond + even(sector), sector)
    bond = loop - even(inner)
    found = []
    if phase == 0:
        if loop % 2 == 0:
            for step, at, size, to in ((-1, 1, 3, 7), (1, 0, 3, 0), (0, 0, 4, 3)):
                found.append(("site", at, size, "left", to, None, home(loop, inner + step)))
        else:
            for step, at, size, to in ((-2, 1, 3, 7), (-1, 0, 4, 3), (0, 0, 3, 0)):
                found.append(("site", at, size, "right", to, None, home(loop - 1, inner + step)))
        for slot, step in enumerate((1, 0, -1)):
            found.append(("notes", 0, 24, "meta", 24 * slot, None, home(loop, inner + step)))
    elif bond % 2 == 0:
        half = (phase - 1) // 2
        if phase % 2 == 1:
            for step, at, size, to in ((2, 1, 2, 1), (2, 3, 1, 6), (1, 0, 1, 0), (1, 1, 2, 4), (1, 3, 1, 9), (0, 0, 1, 3), (0, 1, 2, 7)):
                found.append(("new_right", at, size, "left", to, half, home(bond + 1, inner + step)))
        else:
            if half == 1:
                for step in (0, 1, 2):
                    found.append(("level", 0, 8, "levels", 8 * step, None, home(bond + 1, inner + step)))
                found.append(("level", 0, 8, "weights", 0, None, (bond, inner)))
            for step, at, size, to in ((-2, 1, 3, 7), (-1, 0, 4, 3), (0, 0, 3, 0)):
                found.append(("new_left", at, size, "right", to, half, home(bond - 1, inner + step)))
    elif phase % 2 == 0:
        half = (phase - 1) // 2
        if half == 1:
            found.append(("level", 0, 8, "weights", 0, None, (bond, inner)))
        found.append(("new_left", 0, 4, "sites", 0, half, (bond, inner)))
        for step, at, size in ((2, 3, 1), (1, 1, 2), (0, 0, 1)):
            found.append(("new_right", at, size, "sites", at, half, (bond + 1, inner + step)))
    return [f[:6] + ((f[6][0] - loop, f[6][1] - inner),) for f in found]


def spot_of(source, size, to, where, half):
    return (to, where, size, -1 if half is None else half, source == "new_right")


def part(ref, at, size, source, half):
    if half is None:
        return ref.at[pl.ds(at, size)]
    span = pl.ds(half * (SLOTS // 2), SLOTS // 2)
    return ref.at[pl.ds(at, size), span, :] if source == "new_right" else ref.at[pl.ds(at, size), :, span]


def arrivals(phase, loop, inner):
    found = []
    for far in range(-3, 4):
        for away in range(-3, 4):
            for source, _, size, to, at, half, (x, y) in sends(phase, loop + far, inner + away):
                if (far + x, away + y) == (0, 0):
                    found.append((source, to, at, size, half, (far, away)))
    return found


def kind_of(kind):
    return (4 + kind // 2, 4 + kind % 2)


PHASES = (0, 1, 2, 3, 4)
LANDINGS = sorted({spot_of(a[0], a[3], a[1], a[2], a[4]) for phase in PHASES for kind in range(4) for a in arrivals(phase, *kind_of(kind))})
MOST = max(sum(len(sends(phase, *kind_of(kind))) for phase in PHASES) for kind in range(4))


def partners(loop, inner):
    known = {s[6] for s in sends(0, loop, inner)} | {a[5] for a in arrivals(0, loop, inner)}
    return sorted(known - {(0, 0)})


def by_kind(work):
    loop, inner = lax.axis_index("loop"), lax.axis_index("inner")
    for kind in range(4):
        pl.when((lax.rem(loop, 2) == kind // 2) & (lax.rem(inner, 2) == kind % 2))(functools.partial(work, kind))


def device(offset):
    loop, inner = lax.axis_index("loop"), lax.axis_index("inner")
    rounds, sectors = lax.axis_size("loop"), lax.axis_size("inner")
    return (lax.rem(loop + offset[0] + rounds, rounds), lax.rem(inner + offset[1] + sectors, sectors))


def outgoing(phase, refs, send_sems, recv_sems, kind):
    first = sum(len(sends(p, *kind_of(kind))) for p in range(phase))
    for n, (source, at, size, to, where, half, offset) in enumerate(sends(phase, *kind_of(kind))):
        src, dst = part(refs[source], at, size, source, half), part(refs[to], where, size, source, half)
        slot = recv_sems.at[LANDINGS.index(spot_of(source, size, to, where, half))]
        sem = send_sems.at[first + n]
        yield src, dst, sem, slot, offset


def start(phase, refs, send_sems, recv_sems, kind):
    for src, dst, sem, slot, offset in outgoing(phase, refs, send_sems, recv_sems, kind):
        if offset == (0, 0):
            pltpu.make_async_copy(src, dst, slot).start()
        else:
            pltpu.make_async_remote_copy(src, dst, sem, slot, device_id=device(offset), device_id_type=MESH).start()


def finish(refs, send_sems, recv_sems, kind):
    for phase in PHASES:
        for src, dst, sem, slot, offset in outgoing(phase, refs, send_sems, recv_sems, kind):
            if offset != (0, 0):
                pltpu.make_async_remote_copy(src, dst, sem, slot, device_id=device(offset), device_id_type=MESH).wait_send()


def expect(buffers, refs, recv_sems, kind, halves=(None, 0, 1)):
    for phase in PHASES:
        for source, to, where, size, half, _ in arrivals(phase, *kind_of(kind)):
            if to in buffers and half in halves:
                dst = part(refs[to], where, size, source, half)
                pltpu.make_async_copy(dst, dst, recv_sems.at[LANDINGS.index(spot_of(source, size, to, where, half))]).wait()


def terms_of(outer_a, outer_b):
    found = []
    for d, a, b in PAIRS:
        if CHARGE[a] - CHARGE[outer_a] == d and CHARGE[outer_b] - CHARGE[b] == d:
            found.append(((outer_a * 4 + outer_b) * 16 + a * 4 + b, THETA_AT[d, a, b]))
    return found


def invert_leaf(work):
    n = 128
    lane = lax.broadcasted_iota(jnp.int32, (8, n), 1)
    sub = lax.broadcasted_iota(jnp.int32, (8, n), 0)
    tiles = [work[8 * t:8 * t + 8, :] for t in range(n // 8)]
    for g in range(n // 8):
        k = 8 * g
        cols = {}
        for t in range(g, n // 8):
            cols[t] = [jnp.broadcast_to(tiles[t][:, k + j:k + j + 1], (8, n)) for j in range(8)]
        fresh = (lane >= k) & (lane < k + 8)
        head = jnp.where(fresh, jnp.where(lane - k == sub, 1.0, 0.0), tiles[g])
        for t in range(g + 1, n // 8):
            tiles[t] = jnp.where(fresh, 0.0, tiles[t])
        rows = []
        for j in range(8):
            raw = [jnp.broadcast_to(cols[g][j][i:i + 1, :], (8, n)) for i in range(j, 8)]
            scale = lax.rsqrt(raw[0])
            for t in range(g, n // 8):
                cols[t][j] = cols[t][j] * scale
            low = jnp.where(sub > j, cols[g][j], 0.0)
            for i in range(j + 1, 8):
                other = raw[i - j] * scale
                for t in range(g, n // 8):
                    cols[t][i] = cols[t][i] - cols[t][j] * other
            row = jnp.broadcast_to(head[j:j + 1, :], (8, n)) * scale
            rows.append(row)
            head = jnp.where(sub == j, row, head - low * row)
        tiles[g] = head
        for t in range(g + 1, n // 8):
            total = tiles[t]
            for j in range(8):
                total = total - cols[t][j] * rows[j]
            tiles[t] = total
        work[8 * g:8 * g + 8, :] = jnp.where(lane <= sub + k, head, 0.0)


def body(site, weights_in, gates_in, kept_in, sites, weights_out, left, right, meta, levels, weights, notes, new_left, new_right,
         level, theta, turned, matrix, proj, gram, work, scaled, numbers, lines, table, send_sems, recv_sems, sems):
    n = SLOTS
    h = n // 2
    refs = dict(site=site.at[0, 0], sites=sites.at[0, 0], left=left, right=right, meta=meta, levels=levels, weights=weights,
                notes=notes, new_left=new_left, new_right=new_right, level=level)
    state = (refs, send_sems, recv_sems)
    last = lax.rem(lax.axis_index("loop") + lax.axis_index("inner"), 2) == 0
    small = [
        pltpu.make_async_copy(weights_in.at[0], lines, sems.at[0]),
        pltpu.make_async_copy(gates_in.at[0], table, sems.at[1]),
    ]
    for copy in small:
        copy.start()
    levels[...] = jnp.ones_like(levels)
    barrier = pltpu.get_barrier_semaphore()

    @by_kind
    def _(kind):
        for offset in partners(*kind_of(kind)):
            pl.semaphore_signal(barrier, inc=1, device_id=device(offset), device_id_type=MESH)

    for copy in small:
        copy.wait()
    notes[0:7, :] = jnp.broadcast_to(lines[...], (7, n))
    notes[7:8, :] = jnp.full((1, n), kept_in[0, 0].astype(jnp.float32))
    notes[8:24, :] = jnp.pad(table[...].astype(jnp.bfloat16).astype(jnp.float32), ((0, 0), (0, n - 16)))

    @by_kind
    def _(kind):
        pl.semaphore_wait(barrier, len(partners(*kind_of(kind))))
        start(0, *state, kind)
        expect(("meta",), refs, recv_sems, kind)

    copy = pltpu.make_async_copy(meta.at[pl.ds(24, 24)], numbers, sems.at[2])
    copy.start()

    @by_kind
    def _(kind):
        expect(("left",), refs, recv_sems, kind)

    for d, at in LEFT_AT.items():
        row = meta[24 * (d + 1):24 * (d + 1) + 1, :]
        for k in at.values():
            scaled[k] = (left[k].astype(jnp.float32) * row).astype(jnp.bfloat16)

    for a in range(4):
        turned[a] = left[3 + a].T
    copy.wait()

    for side in range(2):

        @by_kind
        def _(kind):
            expect(("right",), refs, recv_sems, kind, (None, 0) if side == 0 else (1,))

        for d in LEFT_AT:
            wide = jnp.concatenate([right[k, :, side * h:(side + 1) * h] for k in RIGHT_AT[d].values()], axis=1)
            for a, k in LEFT_AT[d].items():
                product = (jnp.dot(scaled[k], wide, preferred_element_type=jnp.float32) * (1.0 / 16.0)).astype(jnp.bfloat16)
                for i, b in enumerate(RIGHT_AT[d]):
                    theta[THETA_AT[d, a, b], :, side * h:(side + 1) * h] = product[:, i * h:(i + 1) * h]

    @pl.loop(0, n // 16)
    def _(step):
        r = pl.multiple_of(step * 16, 16)
        for a in range(4):
            for b in range(4):
                total = None
                for g, t in terms_of(a, b):
                    term = theta[t, pl.ds(r, 16), :].astype(jnp.float32) * numbers[8 + g // 16, g % 16]
                    total = term if total is None else total + term
                matrix[pl.ds(pl.multiple_of(a * n + r, 16), 16), b * n:(b + 1) * n] = total.astype(jnp.bfloat16)

    total = None
    for a in range(4):
        product = jnp.dot(turned[a], matrix[a * n:(a + 1) * n, :], preferred_element_type=jnp.float32)
        total = product if total is None else total + product
    row_number = lax.broadcasted_iota(jnp.int32, (n, 4 * n), 0).astype(jnp.float32)
    proj[...] = jnp.where(row_number < numbers[7, 0], total, 0.0)
    dot = functools.partial(lax.dot_general, precision=HI, preferred_element_type=jnp.float32)
    diagonal = lambda size: lax.broadcasted_iota(jnp.int32, (size, size), 0) == lax.broadcasted_iota(jnp.int32, (size, size), 1)
    upright = lambda row: jnp.sum(jnp.where(diagonal(row.shape[1]), row, 0.0), axis=1, keepdims=True)
    gram[...] = dot(proj[...], proj[...], NT) + jnp.where(diagonal(n), 1.0, 0.0)

    def right_half(half, ortho):
        iso = (ortho * 32.0).astype(jnp.bfloat16)
        for a in range(4):
            new_right[a, half * h:(half + 1) * h, :] = iso[:, a * n:(a + 1) * n]

        @by_kind
        def _(kind):
            start(1 + 2 * half, *state, kind)

        return iso

    def left_half(half, iso):
        span = slice(half * h, (half + 1) * h)
        carried = []
        squares = jnp.zeros((1, h), jnp.float32)
        for a in range(4):
            product = lax.dot_general(matrix[a * n:(a + 1) * n, :], iso, NT, preferred_element_type=jnp.float32) * (1.0 / 32.0)
            carried.append(product)
            squares = squares + jnp.sum(product * product, axis=0, keepdims=True)
        lev = jnp.sqrt(squares * (1.0 / 1024.0) + 1e-6)
        level[:, span] = jnp.broadcast_to(lev, (8, h))
        inverse = 1.0 / lev
        for a in range(4):
            block = (carried[a] * inverse).astype(jnp.bfloat16).astype(jnp.float32)
            new_left[a, :, span] = (block * upright(levels[8 * CHARGE[a]:8 * CHARGE[a] + 1, :])).astype(jnp.bfloat16)

        @pl.when(last)
        def _():
            scale = upright(lev)
            for a in range(4):
                new_right[a, span, :] = (new_right[a, span, :].astype(jnp.float32) * scale).astype(jnp.bfloat16)

        @by_kind
        def _(kind):
            start(2 + 2 * half, *state, kind)

    @by_kind
    def _(kind):
        expect(("levels",), refs, recv_sems, kind)

    work[...] = gram[:h, :h]
    invert_leaf(work)
    first = work[...]
    top = dot(first, proj[:h, :], NN)
    top_iso = right_half(0, top)
    lower = dot(gram[h:, :h], first, NT)
    work[...] = gram[h:, h:] - dot(lower, lower, NT)
    proj[h:, :] = proj[h:, :] - dot(lower, top, NN)
    left_half(0, top_iso)
    invert_leaf(work)
    left_half(1, right_half(1, dot(work[...], proj[h:, :], NN)))

    @by_kind
    def _(kind):
        expect(("weights", "sites"), refs, recv_sems, kind)
        finish(*state, kind)

    weights_out[0] = weights[0:1, :]


def per_device(site_blocks, bond_weights, bond_gates, kept_slots):
    n = SLOTS
    vmem = pl.BlockSpec(memory_space=pltpu.VMEM)
    blocks = lambda count: pltpu.VMEM((count, n, n), jnp.bfloat16)
    rows = lambda count: pltpu.VMEM((count, n), jnp.float32)
    return pl.pallas_call(
        body,
        out_shape=(
            jax.ShapeDtypeStruct(site_blocks.shape, jnp.bfloat16),
            jax.ShapeDtypeStruct(bond_weights.shape, jnp.float32),
        ),
        in_specs=[pl.BlockSpec(memory_space=pltpu.HBM)] * 3 + [pl.BlockSpec(memory_space=pltpu.SMEM)],
        out_specs=(pl.BlockSpec(memory_space=pl.ANY), vmem),
        scratch_shapes=[
            blocks(10), blocks(10), rows(72), rows(24), rows(8), rows(24), blocks(4), blocks(4), rows(8),
            blocks(len(PAIRS)),
            blocks(4),
            pltpu.VMEM((4 * n, 4 * n), jnp.bfloat16),
            pltpu.VMEM((n, 4 * n), jnp.float32),
            pltpu.VMEM((n, n), jnp.float32),
            pltpu.VMEM((n // 2, n // 2), jnp.float32),
            blocks(10),
            pltpu.SMEM((24, n), jnp.float32),
            rows(1),
            pltpu.VMEM((16, 16), jnp.float32),
            pltpu.SemaphoreType.DMA((MOST,)),
            pltpu.SemaphoreType.DMA((len(LANDINGS),)),
            pltpu.SemaphoreType.DMA((3,)),
        ],
        compiler_params=pltpu.CompilerParams(collective_id=0, has_side_effects=True, vmem_limit_bytes=40 << 20),
    )(*[pltpu.with_memory_space_constraint(x, pltpu.HBM) for x in (site_blocks, bond_weights, bond_gates)], kept_slots)


def solution(mesh):
    return jax.shard_map(
        per_device,
        mesh=mesh,
        in_specs=(
            P("loop", "inner", None, None, None),
            P("loop", "inner", None),
            P("loop", None, None),
            P("loop", "inner"),
        ),
        out_specs=(P("loop", "inner", None, None, None), P("loop", "inner", None)),
        check_vma=False,
    )
```

```python
import functools

import jax
import jax.numpy as jnp
from jax import lax
from jax.experimental import pallas as pl
from jax.experimental.pallas import tpu as pltpu
from jax.sharding import PartitionSpec as P

HI = lax.Precision.HIGHEST
NN = (((1,), (0,)), ((), ()))
NT = (((1,), (1,)), ((), ()))
MESH = pl.DeviceIdType.MESH
SLOTS = 256
CHARGE = (0, 1, 1, 2)

LEFT_AT = {-1: {0: 0, 1: 1, 2: 2}, 0: {0: 3, 1: 4, 2: 5, 3: 6}, 1: {1: 7, 2: 8, 3: 9}}
RIGHT_AT = {-1: {1: 1, 2: 2, 3: 6}, 0: {0: 0, 1: 4, 2: 5, 3: 9}, 1: {0: 3, 1: 7, 2: 8}}
PAIRS = [(d, a, b) for d in (-1, 0, 1) for a in LEFT_AT[d] for b in RIGHT_AT[d]]
THETA_AT = {key: n for n, key in enumerate(PAIRS)}


def even(number):
    return 1 - number % 2


def sends(phase, loop, inner):
    home = lambda bond, sector: (bond + even(sector), sector)
    bond = loop - even(inner)
    found = []
    if phase == 0:
        if loop % 2 == 0:
            for step, at, size, to in ((-1, 1, 3, 7), (1, 0, 3, 0), (0, 0, 4, 3)):
                found.append(("site", at, size, "left", to, None, home(loop, inner + step)))
        else:
            for half in (0, 1):
                for step, at, size, to in ((-2, 1, 3, 7), (-1, 0, 4, 3), (0, 0, 3, 0)):
                    found.append(("site", at, size, "right", to, half, home(loop - 1, inner + step)))
        for slot, step in enumerate((1, 0, -1)):
            found.append(("notes", 0, 24, "meta", 24 * slot, None, home(loop, inner + step)))
    elif bond % 2 == 0:
        half = (phase - 1) // 2
        if phase % 2 == 1:
            for step, at, size, to in ((2, 1, 2, 1), (2, 3, 1, 6), (1, 0, 1, 0), (1, 1, 2, 4), (1, 3, 1, 9), (0, 0, 1, 3), (0, 1, 2, 7)):
                found.append(("new_right", at, size, "left", to, half, home(bond + 1, inner + step)))
        else:
            if half == 1:
                for step in (0, 1, 2):
                    found.append(("level", 0, 8, "levels", 8 * step, None, home(bond + 1, inner + step)))
                found.append(("level", 0, 8, "weights", 0, None, (bond, inner)))
            for step, at, size, to in ((-2, 1, 3, 7), (-1, 0, 4, 3), (0, 0, 3, 0)):
                found.append(("new_left", at, size, "right", to, half, home(bond - 1, inner + step)))
    elif phase % 2 == 0:
        half = (phase - 1) // 2
        if half == 1:
            found.append(("level", 0, 8, "weights", 0, None, (bond, inner)))
        found.append(("new_left", 0, 4, "sites", 0, half, (bond, inner)))
        for step, at, size in ((2, 3, 1), (1, 1, 2), (0, 0, 1)):
            found.append(("new_right", at, size, "sites", at, half, (bond + 1, inner + step)))
    return [f[:6] + ((f[6][0] - loop, f[6][1] - inner),) for f in found]


def spot_of(source, size, to, where, half):
    return (to, where, size, -1 if half is None else half, source == "new_right")


def part(refs, name, at, size, source, half):
    ref = refs[name]
    if half is None:
        return ref.at[pl.ds(at, size)]
    if name in ("new_left", "right"):
        return ref.at[half, pl.ds(at, size)]
    span = pl.ds(half * (SLOTS // 2), SLOTS // 2)
    return ref.at[pl.ds(at, size), span, :] if source == "new_right" else ref.at[pl.ds(at, size), :, span]


def arrivals(phase, loop, inner):
    found = []
    for far in range(-3, 4):
        for away in range(-3, 4):
            for source, _, size, to, at, half, (x, y) in sends(phase, loop + far, inner + away):
                if (far + x, away + y) == (0, 0):
                    found.append((source, to, at, size, half, (far, away)))
    return found


def kind_of(kind):
    return (4 + kind // 2, 4 + kind % 2)


PHASES = (0, 1, 2, 3, 4)
LANDINGS = sorted({spot_of(a[0], a[3], a[1], a[2], a[4]) for phase in PHASES for kind in range(4) for a in arrivals(phase, *kind_of(kind))})
MOST = max(sum(len(sends(phase, *kind_of(kind))) for phase in PHASES) for kind in range(4))


def partners(loop, inner):
    known = {s[6] for s in sends(0, loop, inner)} | {a[5] for a in arrivals(0, loop, inner)}
    return sorted(known - {(0, 0)})


def by_kind(work):
    loop, inner = lax.axis_index("loop"), lax.axis_index("inner")
    for kind in range(4):
        pl.when((lax.rem(loop, 2) == kind // 2) & (lax.rem(inner, 2) == kind % 2))(functools.partial(work, kind))


def device(offset):
    loop, inner = lax.axis_index("loop"), lax.axis_index("inner")
    rounds, sectors = lax.axis_size("loop"), lax.axis_size("inner")
    return (lax.rem(loop + offset[0] + rounds, rounds), lax.rem(inner + offset[1] + sectors, sectors))


def outgoing(phase, refs, send_sems, recv_sems, kind):
    first = sum(len(sends(p, *kind_of(kind))) for p in range(phase))
    for n, (source, at, size, to, where, half, offset) in enumerate(sends(phase, *kind_of(kind))):
        src, dst = part(refs, source, at, size, source, half), part(refs, to, where, size, source, half)
        slot = recv_sems.at[LANDINGS.index(spot_of(source, size, to, where, half))]
        sem = send_sems.at[first + n]
        yield src, dst, sem, slot, offset


def start(phase, refs, send_sems, recv_sems, kind):
    for src, dst, sem, slot, offset in outgoing(phase, refs, send_sems, recv_sems, kind):
        if offset == (0, 0):
            pltpu.make_async_copy(src, dst, slot).start()
        else:
            pltpu.make_async_remote_copy(src, dst, sem, slot, device_id=device(offset), device_id_type=MESH).start()


def finish(refs, send_sems, recv_sems, kind):
    for phase in PHASES:
        for src, dst, sem, slot, offset in outgoing(phase, refs, send_sems, recv_sems, kind):
            if offset != (0, 0):
                pltpu.make_async_remote_copy(src, dst, sem, slot, device_id=device(offset), device_id_type=MESH).wait_send()


def expect(buffers, refs, recv_sems, kind, halves=(None, 0, 1)):
    for phase in PHASES:
        for source, to, where, size, half, _ in arrivals(phase, *kind_of(kind)):
            if to in buffers and half in halves:
                dst = part(refs, to, where, size, source, half)
                pltpu.make_async_copy(dst, dst, recv_sems.at[LANDINGS.index(spot_of(source, size, to, where, half))]).wait()


def terms_of(outer_a, outer_b):
    found = []
    for d, a, b in PAIRS:
        if CHARGE[a] - CHARGE[outer_a] == d and CHARGE[outer_b] - CHARGE[b] == d:
            found.append(((outer_a * 4 + outer_b) * 16 + a * 4 + b, THETA_AT[d, a, b]))
    return found


def invert_leaf(work):
    n = 128
    lane = lax.broadcasted_iota(jnp.int32, (8, n), 1)
    sub = lax.broadcasted_iota(jnp.int32, (8, n), 0)
    tiles = [work[8 * t:8 * t + 8, :] for t in range(n // 8)]
    for g in range(n // 8):
        k = 8 * g
        cols = {}
        for t in range(g, n // 8):
            cols[t] = [jnp.broadcast_to(tiles[t][:, k + j:k + j + 1], (8, n)) for j in range(8)]
        fresh = (lane >= k) & (lane < k + 8)
        head = jnp.where(fresh, jnp.where(lane - k == sub, 1.0, 0.0), tiles[g])
        for t in range(g + 1, n // 8):
            tiles[t] = jnp.where(fresh, 0.0, tiles[t])
        rows = []
        for j in range(8):
            raw = [jnp.broadcast_to(cols[g][j][i:i + 1, :], (8, n)) for i in range(j, 8)]
            scale = lax.rsqrt(raw[0])
            for t in range(g, n // 8):
                cols[t][j] = cols[t][j] * scale
            low = jnp.where(sub > j, cols[g][j], 0.0)
            for i in range(j + 1, 8):
                other = raw[i - j] * scale
                for t in range(g, n // 8):
                    cols[t][i] = cols[t][i] - cols[t][j] * other
            row = jnp.broadcast_to(head[j:j + 1, :], (8, n)) * scale
            rows.append(row)
            head = jnp.where(sub == j, row, head - low * row)
        tiles[g] = head
        for t in range(g + 1, n // 8):
            total = tiles[t]
            for j in range(8):
                total = total - cols[t][j] * rows[j]
            tiles[t] = total
        work[8 * g:8 * g + 8, :] = jnp.where(lane <= sub + k, head, 0.0)


def body(site, weights_in, gates_in, kept_in, sites, weights_out, left, right, meta, levels, weights, notes, new_left, new_right,
         level, theta, turned, matrix, proj, gram, work, scaled, numbers, lines, table, send_sems, recv_sems, sems):
    n = SLOTS
    h = n // 2
    refs = dict(site=site.at[0, 0], sites=sites.at[0, 0], left=left, right=right, meta=meta, levels=levels, weights=weights,
                notes=notes, new_left=new_left, new_right=new_right, level=level)
    state = (refs, send_sems, recv_sems)
    last = lax.rem(lax.axis_index("loop") + lax.axis_index("inner"), 2) == 0
    small = [
        pltpu.make_async_copy(weights_in.at[0], lines, sems.at[0]),
        pltpu.make_async_copy(gates_in.at[0], table, sems.at[1]),
    ]
    for copy in small:
        copy.start()
    levels[...] = jnp.ones_like(levels)
    barrier = pltpu.get_barrier_semaphore()

    @by_kind
    def _(kind):
        for offset in partners(*kind_of(kind)):
            pl.semaphore_signal(barrier, inc=1, device_id=device(offset), device_id_type=MESH)

    for copy in small:
        copy.wait()
    notes[0:7, :] = jnp.broadcast_to(lines[...], (7, n))
    notes[7:8, :] = jnp.full((1, n), kept_in[0, 0].astype(jnp.float32))
    notes[8:24, :] = jnp.pad(table[...].astype(jnp.bfloat16).astype(jnp.float32), ((0, 0), (0, n - 16)))

    @by_kind
    def _(kind):
        pl.semaphore_wait(barrier, len(partners(*kind_of(kind))))
        start(0, *state, kind)
        expect(("meta",), refs, recv_sems, kind)

    copy = pltpu.make_async_copy(meta.at[pl.ds(24, 24)], numbers, sems.at[2])
    copy.start()

    @by_kind
    def _(kind):
        expect(("left",), refs, recv_sems, kind)

    for d, at in LEFT_AT.items():
        row = meta[24 * (d + 1):24 * (d + 1) + 1, :]
        for k in at.values():
            scaled[k] = (left[k].astype(jnp.float32) * row).astype(jnp.bfloat16)

    for a in range(4):
        turned[a] = left[3 + a].T
    copy.wait()

    for side in range(2):

        @by_kind
        def _(kind):
            expect(("right",), refs, recv_sems, kind, (side,))

        for d in LEFT_AT:
            wide = jnp.concatenate([right[side, k] for k in RIGHT_AT[d].values()], axis=1)
            for a, k in LEFT_AT[d].items():
                product = (jnp.dot(scaled[k], wide, preferred_element_type=jnp.float32) * (1.0 / 16.0)).astype(jnp.bfloat16)
                for i, b in enumerate(RIGHT_AT[d]):
                    theta[THETA_AT[d, a, b], :, side * h:(side + 1) * h] = product[:, i * h:(i + 1) * h]

    @pl.loop(0, n // 16)
    def _(step):
        r = pl.multiple_of(step * 16, 16)
        for a in range(4):
            for b in range(4):
                total = None
                for g, t in terms_of(a, b):
                    term = theta[t, pl.ds(r, 16), :].astype(jnp.float32) * numbers[8 + g // 16, g % 16]
                    total = term if total is None else total + term
                matrix[pl.ds(pl.multiple_of(a * n + r, 16), 16), b * n:(b + 1) * n] = total.astype(jnp.bfloat16)

    total = None
    for a in range(4):
        product = jnp.dot(turned[a], matrix[a * n:(a + 1) * n, :], preferred_element_type=jnp.float32)
        total = product if total is None else total + product
    row_number = lax.broadcasted_iota(jnp.int32, (n, 4 * n), 0).astype(jnp.float32)
    proj[...] = jnp.where(row_number < numbers[7, 0], total, 0.0)
    dot = functools.partial(lax.dot_general, precision=HI, preferred_element_type=jnp.float32)
    diagonal = lambda size: lax.broadcasted_iota(jnp.int32, (size, size), 0) == lax.broadcasted_iota(jnp.int32, (size, size), 1)
    upright = lambda row: jnp.sum(jnp.where(diagonal(row.shape[1]), row, 0.0), axis=1, keepdims=True)
    gram[...] = dot(proj[...], proj[...], NT) + jnp.where(diagonal(n), 1.0, 0.0)

    def right_half(half, ortho):
        iso = (ortho * 32.0).astype(jnp.bfloat16)
        for a in range(4):
            new_right[a, half * h:(half + 1) * h, :] = iso[:, a * n:(a + 1) * n]

        @by_kind
        def _(kind):
            start(1 + 2 * half, *state, kind)

        return iso

    def left_half(half, iso):
        span = slice(half * h, (half + 1) * h)
        carried = []
        squares = jnp.zeros((1, h), jnp.float32)
        for a in range(4):
            product = lax.dot_general(matrix[a * n:(a + 1) * n, :], iso, NT, preferred_element_type=jnp.float32) * (1.0 / 32.0)
            carried.append(product)
            squares = squares + jnp.sum(product * product, axis=0, keepdims=True)
        lev = jnp.sqrt(squares * (1.0 / 1024.0) + 1e-6)
        level[:, span] = jnp.broadcast_to(lev, (8, h))
        inverse = 1.0 / lev
        for a in range(4):
            block = (carried[a] * inverse).astype(jnp.bfloat16).astype(jnp.float32)
            new_left[half, a] = (block * upright(levels[8 * CHARGE[a]:8 * CHARGE[a] + 1, :])).astype(jnp.bfloat16)

        @pl.when(last)
        def _():
            scale = upright(lev)
            for a in range(4):
                new_right[a, span, :] = (new_right[a, span, :].astype(jnp.float32) * scale).astype(jnp.bfloat16)

        @by_kind
        def _(kind):
            start(2 + 2 * half, *state, kind)

    @by_kind
    def _(kind):
        expect(("levels",), refs, recv_sems, kind)

    work[...] = gram[:h, :h]
    invert_leaf(work)
    first = work[...]
    top = dot(first, proj[:h, :], NN)
    left_half(0, right_half(0, top))
    lower = dot(gram[h:, :h], first, NT)
    work[...] = gram[h:, h:] - dot(lower, lower, NT)
    proj[h:, :] = proj[h:, :] - dot(lower, top, NN)
    invert_leaf(work)
    left_half(1, right_half(1, dot(work[...], proj[h:, :], NN)))

    @by_kind
    def _(kind):
        expect(("weights", "sites"), refs, recv_sems, kind)
        finish(*state, kind)

    weights_out[0] = weights[0:1, :]


def per_device(site_blocks, bond_weights, bond_gates, kept_slots):
    n = SLOTS
    vmem = pl.BlockSpec(memory_space=pltpu.VMEM)
    blocks = lambda count: pltpu.VMEM((count, n, n), jnp.bfloat16)
    rows = lambda count: pltpu.VMEM((count, n), jnp.float32)
    return pl.pallas_call(
        body,
        out_shape=(
            jax.ShapeDtypeStruct(site_blocks.shape, jnp.bfloat16),
            jax.ShapeDtypeStruct(bond_weights.shape, jnp.float32),
        ),
        in_specs=[pl.BlockSpec(memory_space=pltpu.HBM)] * 3 + [pl.BlockSpec(memory_space=pltpu.SMEM)],
        out_specs=(pl.BlockSpec(memory_space=pl.ANY), vmem),
        scratch_shapes=[
            blocks(10), pltpu.VMEM((2, 10, n, n // 2), jnp.bfloat16), rows(72), rows(24), rows(8), rows(24),
            pltpu.VMEM((2, 4, n, n // 2), jnp.bfloat16), blocks(4), rows(8),
            blocks(len(PAIRS)),
            blocks(4),
            pltpu.VMEM((4 * n, 4 * n), jnp.bfloat16),
            pltpu.VMEM((n, 4 * n), jnp.float32),
            pltpu.VMEM((n, n), jnp.float32),
            pltpu.VMEM((n // 2, n // 2), jnp.float32),
            blocks(10),
            pltpu.SMEM((24, n), jnp.float32),
            rows(1),
            pltpu.VMEM((16, 16), jnp.float32),
            pltpu.SemaphoreType.DMA((MOST,)),
            pltpu.SemaphoreType.DMA((len(LANDINGS),)),
            pltpu.SemaphoreType.DMA((3,)),
        ],
        compiler_params=pltpu.CompilerParams(collective_id=0, has_side_effects=True, vmem_limit_bytes=40 << 20),
    )(*[pltpu.with_memory_space_constraint(x, pltpu.HBM) for x in (site_blocks, bond_weights, bond_gates)], kept_slots)


def solution(mesh):
    return jax.shard_map(
        per_device,
        mesh=mesh,
        in_specs=(
            P("loop", "inner", None, None, None),
            P("loop", "inner", None),
            P("loop", None, None),
            P("loop", "inner"),
        ),
        out_specs=(P("loop", "inner", None, None, None), P("loop", "inner", None)),
        check_vma=False,
    )
```
